32 devices in a mesh: fsdp: 4 (over y, x), ctx: 4 (over z), tp: 2 (over core).
Axes of the slice: x: 2, y: 2, z: 4, core: 2. Of those that a mesh axis runs over, the one named last changes fastest.
Arguments:
- layer_input: float32 [4, 2048, 2048], P('fsdp', 'ctx'), may hold values from -6 to 6
- cot: float32 [4, 2048, 2048], P('fsdp', 'ctx'), may hold values from -6 to 6
- wq: bfloat16 [2048, 2048], P('fsdp', 'tp'), may hold values from -0.125 to 0.125
- wk: bfloat16 [2048, 256], P('fsdp', 'tp'), may hold values from -0.125 to 0.125
- wv: bfloat16 [2048, 256], P('fsdp', 'tp'), may hold values from -0.125 to 0.125
- wo: bfloat16 [2048, 2048], P('tp', 'fsdp'), may hold values from -0.75 to 0.75
- w_gate: bfloat16 [2048, 5632], P('fsdp', 'tp'), may hold values from -0.125 to 0.125
- w_up: bfloat16 [2048, 5632], P('fsdp', 'tp'), may hold values from -0.125 to 0.125
- w_down: bfloat16 [5632, 2048], P('tp', 'fsdp'), may hold values from -0.078125 to 0.078125
- gain_attn: bfloat16 [2048], P('fsdp'), may hold values from 0.5 to 1.5
- gain_mlp: bfloat16 [2048], P('fsdp'), may hold values from 0.5 to 1.5
Outputs:
- layer_output: float32 [4, 2048, 2048], P('fsdp', 'ctx')
- dx: float32 [4, 2048, 2048], P('fsdp', 'ctx')
- dwq: float32 [2048, 2048], P('fsdp', 'tp')
- dwk: float32 [2048, 256], P('fsdp', 'tp')
- dwv: float32 [2048, 256], P('fsdp', 'tp')
- dwo: float32 [2048, 2048], P('tp', 'fsdp')
- dw_gate: float32 [2048, 5632], P('fsdp', 'tp')
- dw_up: float32 [2048, 5632], P('fsdp', 'tp')
- dw_down: float32 [5632, 2048], P('tp', 'fsdp')
- dgain_attn: float32 [2048], P('fsdp')
- dgain_mlp: float32 [2048], P('fsdp')
The draws below stay inside these ranges and needn't reach their ends.
All inputs are finite; a program needn't handle non-finite values.
Results may differ from the reference program's by a relative error of at most 0.02.
Values may be sent and summed in bfloat16 or wider, within the bound.
No kernel may reach another device: no remote copies, remote signals or barrier semaphores. Data moves between devices by JAX's collectives and lax.ppermute only.
A program may use at most 320 MiB of HBM per device.

```python
import jax
import jax.numpy as jnp
from jax import lax

D = 2048
H = 32
KV = 4
HD = 64
FF = 5632
L = 2048
SEQS = 4


def levels(own_key, dims, cuts, least, high):
    def one(position, blocks):
        heights = jax.random.uniform(jax.random.fold_in(jax.random.fold_in(own_key, 6), position), (blocks,), jnp.float32, least / len(cuts), high / len(cuts))
        return jnp.repeat(jnp.exp(heights), dims[position] // blocks).reshape((-1,) + (1,) * (len(dims) - position - 1))

    factor_of = one(*cuts[0])
    for cut in cuts[1:]:
        factor_of = factor_of * one(*cut)
    return factor_of


def normal_values(key, shape, deviation, bound, shards=(), kind=jnp.bfloat16):
    factor_of = levels(key, shape, shards, -0.22, 0.18) if shards else 1.0
    entries = jax.random.normal(key, shape, jnp.float32) * deviation * factor_of
    return jnp.minimum(jnp.maximum(entries, -bound), bound).astype(kind)


def setup_inputs(seed: int = 0) -> dict:
    streams_of = jax.random.split(jax.random.key(seed), 12)
    return {
        "layer_input": normal_values(streams_of[0], (SEQS, L, D), 1.0, 6.0, ((0, 4), (1, 4)), jnp.float32),
        "cot": normal_values(streams_of[1], (SEQS, L, D), 1.0, 6.0, ((0, 4), (1, 4)), jnp.float32),
        "wq": normal_values(streams_of[2], (D, H * HD), D ** -0.5, 0.125, ((0, 4), (1, 2))),
        "wk": normal_values(streams_of[3], (D, KV * HD), D ** -0.5, 0.125, ((0, 4), (1, 2))),
        "wv": normal_values(streams_of[4], (D, KV * HD), D ** -0.5, 0.125, ((0, 4), (1, 2))),
        "wo": normal_values(streams_of[5], (H * HD, D), HD ** -0.5, 0.75, ((0, 2), (1, 4))),
        "w_gate": normal_values(streams_of[6], (D, FF), D ** -0.5, 0.125, ((0, 4), (1, 2))),
        "w_up": normal_values(streams_of[7], (D, FF), D ** -0.5, 0.125, ((0, 4), (1, 2))),
        "w_down": normal_values(streams_of[8], (FF, D), FF ** -0.5, 0.078125, ((0, 2), (1, 4))),
        "gain_attn": jnp.clip(1.0 + 0.1 * jax.random.normal(streams_of[9], (D,), jnp.float32), 0.5, 1.5).astype(jnp.bfloat16),
        "gain_mlp": jnp.clip(1.0 + 0.1 * jax.random.normal(streams_of[10], (D,), jnp.float32), 0.5, 1.5).astype(jnp.bfloat16),
    }


EPS = 1e-05
ROPE_BASE = 10000.0
NEG_BIG = -1e+30

def rope_tables(positions, head_dim):
    half = head_dim // 2
    freq = ROPE_BASE ** (-(jnp.arange(half, dtype=jnp.float32) * 2.0 / head_dim))
    angles = positions.astype(jnp.float32)[:, None] * freq[None, :]
    cosine = jnp.concatenate([jnp.cos(angles), jnp.cos(angles)], -1)
    sine = jnp.concatenate([jnp.sin(angles), jnp.sin(angles)], -1)
    return (cosine, sine)

def rotate_half(values):
    half = values.shape[-1] // 2
    return jnp.concatenate([-values[..., half:], values[..., :half]], -1)

def rope_apply(values, cosine, sine):
    return values * cosine[:, None, :] + rotate_half(values) * sine[:, None, :]

def rope_undo(grads, cosine, sine):
    return grads * cosine[:, None, :] - rotate_half(grads * sine[:, None, :])

def norm_forward(hidden, gain):
    inverse = lax.rsqrt(lax.optimization_barrier(jnp.mean(hidden * hidden, -1, keepdims=True)) + EPS)
    normal = hidden * inverse
    return (normal, inverse, (normal * gain).astype(jnp.bfloat16))

def norm_backward(grad_normed, normal, inverse, gain):
    scaled = grad_normed * gain
    grad_in = inverse * (scaled - normal * lax.optimization_barrier(jnp.mean(scaled * normal, -1, keepdims=True)))
    return (grad_in, lax.optimization_barrier(jnp.sum(grad_normed * normal, 0)))

def to_bf_and_back(values):
    return lax.optimization_barrier(values.astype(jnp.bfloat16)).astype(jnp.float32)

def one_sequence(hidden_in, upstream, weights):
    wq, wk, wv, wo, w_gate, w_up, w_down, gain_one, gain_two = weights
    seq_len = hidden_in.shape[0]
    heads = wq.shape[1] // HD
    kv_heads = wk.shape[1] // HD
    group = heads // kv_heads
    scale = 1.0 / HD ** 0.5
    qrows = min(512, seq_len)
    nblocks = seq_len // qrows
    positions = jnp.arange(seq_len, dtype=jnp.int32)
    cosine, sine = rope_tables(positions, HD)
    normal_one, inv_one, normed_one = norm_forward(hidden_in, gain_one)
    queries = rope_apply(jnp.dot(normed_one, wq, preferred_element_type=jnp.float32).reshape(seq_len, heads, HD), cosine, sine)
    queries = queries.astype(jnp.bfloat16).reshape(seq_len, kv_heads, group, HD)
    keys = rope_apply(jnp.dot(normed_one, wk, preferred_element_type=jnp.float32).reshape(seq_len, kv_heads, HD), cosine, sine).astype(jnp.bfloat16)
    values = jnp.dot(normed_one, wv, preferred_element_type=jnp.float32).astype(jnp.bfloat16).reshape(seq_len, kv_heads, HD)
    keys_f = keys.astype(jnp.float32)
    values_f = values.astype(jnp.float32)

    def block_probs(index):
        start = index * qrows
        qblock = lax.dynamic_slice_in_dim(queries, start, qrows, 0).astype(jnp.float32)
        scores = jnp.einsum('qkgd,skd->kgqs', qblock, keys_f) * scale
        qpos = start + jnp.arange(qrows, dtype=jnp.int32)
        visible = positions[None, :] <= qpos[:, None]
        masked = jnp.where(visible, scores, NEG_BIG)
        top = lax.optimization_barrier(jnp.max(masked, -1, keepdims=True))
        total = lax.optimization_barrier(jnp.sum(jnp.where(visible, jnp.exp(scores - top), 0.0), -1, keepdims=True))
        lse = top + jnp.log(total)
        probs = jnp.where(visible, jnp.exp(scores - lse), 0.0)
        return (qblock, probs, lse)

    def attend(index):
        qblock, probs, lse = block_probs(index)
        context = jnp.einsum('kgqs,skd->qkgd', to_bf_and_back(probs), values_f)
        return (context.astype(jnp.bfloat16), lse)
    context, lse_all = lax.map(attend, jnp.arange(nblocks, dtype=jnp.int32))
    context = context.reshape(seq_len, heads * HD)
    mid = hidden_in + jnp.dot(context, wo, preferred_element_type=jnp.float32)
    normal_two, inv_two, normed_two = norm_forward(mid, gain_two)
    gate = jnp.dot(normed_two, w_gate, preferred_element_type=jnp.float32)
    up = jnp.dot(normed_two, w_up, preferred_element_type=jnp.float32)
    sig = jax.nn.sigmoid(gate)
    silu = gate * sig
    act = (silu * up).astype(jnp.bfloat16)
    block_out = mid + jnp.dot(act, w_down, preferred_element_type=jnp.float32)
    cot_b = upstream.astype(jnp.bfloat16)
    d_act = jnp.dot(cot_b, w_down.T, preferred_element_type=jnp.float32)
    d_gate = (d_act * up * sig * (1.0 + gate * (1.0 - sig))).astype(jnp.bfloat16)
    d_up = (d_act * silu).astype(jnp.bfloat16)
    dw_down = jnp.dot(act.T, cot_b, preferred_element_type=jnp.float32)
    dw_gate = jnp.dot(normed_two.T, d_gate, preferred_element_type=jnp.float32)
    dw_up = jnp.dot(normed_two.T, d_up, preferred_element_type=jnp.float32)
    dn_two = jnp.dot(d_gate, w_gate.T, preferred_element_type=jnp.float32) + jnp.dot(d_up, w_up.T, preferred_element_type=jnp.float32)
    back_two, dgain_two = norm_backward(dn_two, normal_two, inv_two, gain_two)
    dmid = upstream + back_two
    dmid_b = dmid.astype(jnp.bfloat16)
    dwo = jnp.dot(context.T, dmid_b, preferred_element_type=jnp.float32)
    d_context = jnp.dot(dmid_b, wo.T, preferred_element_type=jnp.float32).astype(jnp.bfloat16)
    d_context4 = d_context.reshape(seq_len, kv_heads, group, HD)
    context4 = context.reshape(seq_len, kv_heads, group, HD)

    def back_block(carry, index):
        dk_sum, dv_sum = carry
        qblock, probs, lse = block_probs(index)
        start = index * qrows
        dout = lax.dynamic_slice_in_dim(d_context4, start, qrows, 0).astype(jnp.float32)
        cblock = lax.dynamic_slice_in_dim(context4, start, qrows, 0).astype(jnp.float32)
        delta = jnp.transpose(lax.optimization_barrier(jnp.sum(dout * cblock, -1)), (1, 2, 0))
        dv_sum = dv_sum + jnp.einsum('kgqs,qkgd->skd', to_bf_and_back(probs), dout)
        dprobs = jnp.einsum('qkgd,skd->kgqs', dout, values_f)
        dscores = to_bf_and_back(probs * (dprobs - delta[..., None]) * scale)
        dq_block = jnp.einsum('kgqs,skd->qkgd', dscores, keys_f)
        dk_sum = dk_sum + jnp.einsum('kgqs,qkgd->skd', dscores, qblock)
        return ((dk_sum, dv_sum), dq_block)
    zeros_kv = jnp.zeros((seq_len, kv_heads, HD), jnp.float32)
    (dk_rot, dv_sum), dq_rot = lax.scan(back_block, (zeros_kv, zeros_kv), jnp.arange(nblocks, dtype=jnp.int32))
    dq_rot = dq_rot.reshape(seq_len, heads, HD)
    dq = rope_undo(dq_rot, cosine, sine).astype(jnp.bfloat16).reshape(seq_len, heads * HD)
    dk = rope_undo(dk_rot, cosine, sine).astype(jnp.bfloat16).reshape(seq_len, kv_heads * HD)
    dv_b = dv_sum.astype(jnp.bfloat16).reshape(seq_len, kv_heads * HD)
    dwq = jnp.dot(normed_one.T, dq, preferred_element_type=jnp.float32)
    dwk = jnp.dot(normed_one.T, dk, preferred_element_type=jnp.float32)
    dwv = jnp.dot(normed_one.T, dv_b, preferred_element_type=jnp.float32)
    dn_one = jnp.dot(dq, wq.T, preferred_element_type=jnp.float32) + jnp.dot(dk, wk.T, preferred_element_type=jnp.float32) + jnp.dot(dv_b, wv.T, preferred_element_type=jnp.float32)
    back_one, dgain_one = norm_backward(dn_one, normal_one, inv_one, gain_one)
    grad_input = dmid + back_one
    return (block_out, grad_input, (dwq, dwk, dwv, dwo, dw_gate, dw_up, dw_down, dgain_one, dgain_two))

def reference(layer_input, cot, wq, wk, wv, wo, w_gate, w_up, w_down, gain_attn, gain_mlp):
    weights = (wq, wk, wv, wo, w_gate, w_up, w_down, gain_attn.astype(jnp.float32), gain_mlp.astype(jnp.float32))
    shapes = [wq.shape, wk.shape, wv.shape, wo.shape, w_gate.shape, w_up.shape, w_down.shape, gain_attn.shape, gain_mlp.shape]
    init = tuple((jnp.zeros(shape, jnp.float32) for shape in shapes))

    def step(carry, inputs):
        hidden_in, upstream = inputs
        block_out, grad_input, grads = one_sequence(hidden_in, upstream, weights)
        return (tuple((total + part for total, part in zip(carry, grads))), (block_out, grad_input))
    grads, (layer_output, grad_inputs) = lax.scan(step, init, (layer_input, cot))
    return (layer_output, grad_inputs, grads[0], grads[1], grads[2], grads[3], grads[4], grads[5], grads[6], grads[7], grads[8])
```

```python
import functools
import math

import jax
import jax.numpy as jnp
from jax import lax
from jax.experimental import pallas as pl
from jax.experimental.pallas import tpu as pltpu
from jax.sharding import PartitionSpec as P

HD = 64
EPS = 1e-05
ROPE_BASE = 10000.0
NEG_BIG = -1e30
F32 = jnp.float32
BF16 = jnp.bfloat16


LOG2E = 1.4426950408889634
VMEM_LIMIT = 56 * 1024 * 1024


def rope_tables(positions, head_dim):
    half = head_dim // 2
    freq = ROPE_BASE ** (-(jnp.arange(half, dtype=F32) * 2.0 / head_dim))
    angles = positions.astype(F32)[None, :] * freq[:, None]
    return (jnp.cos(angles), jnp.sin(angles))


def rope(values, cosine, sine):
    rows, tokens = values.shape
    first, second = jnp.moveaxis(values.reshape(rows // HD, 2, HD // 2, tokens), 1, 0)
    turned = [first * cosine - second * sine, second * cosine + first * sine]
    return jnp.stack(turned, 1).reshape(rows, tokens)


def dot(left, right, dims):
    return lax.dot_general(left, right, ((dims[:1], dims[1:]), ((), ())), preferred_element_type=F32)


def causal(shape):
    keys = lax.broadcasted_iota(jnp.int32, shape, 0)
    return keys <= lax.broadcasted_iota(jnp.int32, shape, 1)


def attend_kernel(factor, heads, index, q_ref, k_ref, vt_ref, out_ref, lse_ref):
    last = index[0]

    def step(back, carry, masked):
        after_step = []
        for h, (top, total, accum) in enumerate(carry):
            scores = dot(k_ref[back, 0], q_ref[pl.ds(h * HD, HD), :], (1, 0))
            if masked:
                scores = jnp.where(causal(scores.shape), scores, NEG_BIG)
            newest = jnp.maximum(top, jnp.max(scores, 0, keepdims=True))
            probs = jnp.exp2((scores - newest) * factor)
            fade = jnp.exp2((top - newest) * factor)
            total = total * fade + jnp.sum(probs, 0, keepdims=True)
            accum = accum * fade + dot(vt_ref[back, 0], probs.astype(BF16), (1, 0))
            after_step.append((newest, total, accum))
        return tuple(after_step)

    tokens = q_ref.shape[1]
    row = jnp.zeros((1, tokens), F32)
    carry = tuple((row + NEG_BIG, row, jnp.zeros((HD, tokens), F32)) for _ in range(heads))
    carry = step(0, carry, True)
    carry = lax.fori_loop(1, last + 1, functools.partial(step, masked=False), carry)
    for h, (top, total, accum) in enumerate(carry):
        out_ref[pl.ds(h * HD, HD), :] = (accum / total).astype(BF16)
        lse_ref[h] = top * factor + jnp.log(total) * LOG2E


def attend_back_kernel(
    factor, heads, chunks, index, q_ref, do_ref, o_ref, lse_ref, k_ref, v_ref, kt_ref, dq_ref, dk_ref, dv_ref
):
    last = index[0]
    rows = [pl.ds(h * HD, HD) for h in range(heads)]
    deltas = [
        jnp.sum(do_ref[r, :].astype(F32) * o_ref[r, :].astype(F32), 0, keepdims=True) for r in rows
    ]

    @pl.when(pl.program_id(0) % chunks == 0)
    def _():
        dk_ref[...] = jnp.zeros_like(dk_ref)
        dv_ref[...] = jnp.zeros_like(dv_ref)

    def step(back, masked):
        dk, dv = dk_ref[back, 0], dv_ref[back, 0]
        for h, r in enumerate(rows):
            q, do = q_ref[r, :], do_ref[r, :]
            scores = dot(k_ref[back, 0], q, (1, 0))
            probs = jnp.exp2(scores * factor - lse_ref[h])
            if masked:
                probs = jnp.where(causal(scores.shape), probs, 0.0)
            dv = dv + dot(probs.astype(BF16), do, (1, 1))
            dprobs = dot(v_ref[back, 0], do, (1, 0))
            dscores = (probs * (dprobs - deltas[h])).astype(BF16)
            dk = dk + dot(dscores, q, (1, 1))
            dq = dot(kt_ref[back, 0], dscores, (1, 0))
            if masked:
                dq_ref[r, :] = dq
            else:
                dq_ref[r, :] += dq
        dk_ref[back, 0] = dk
        dv_ref[back, 0] = dv

    step(0, True)

    def body(back, carry):
        step(back, False)
        return carry

    lax.fori_loop(1, last + 1, body, 0)


def heads_at_once(group):
    return max(n for n in (4, 2, 1) if group % n == 0)


def attend(index, queries, keys, values_t):
    blocks, kv, tokens, _ = keys.shape
    q_rows = queries.shape[0]
    group = q_rows // HD // kv
    heads = heads_at_once(group)
    chunks = group // heads
    per_head = pl.BlockSpec((heads * HD, tokens), lambda i, c: (i, 0))
    work = blocks * tokens * tokens * (q_rows // HD)
    return pl.pallas_call(
        functools.partial(attend_kernel, LOG2E / math.sqrt(HD), heads),
        out_shape=(
            jax.ShapeDtypeStruct(queries.shape, BF16),
            jax.ShapeDtypeStruct((q_rows // HD, 1, tokens), F32),
        ),
        grid_spec=pltpu.PrefetchScalarGridSpec(
            num_scalar_prefetch=1,
            grid=(kv * chunks,),
            in_specs=[
                per_head,
                pl.BlockSpec((blocks, 1, tokens, HD), lambda i, c: (0, i // chunks, 0, 0)),
                pl.BlockSpec((blocks, 1, HD, tokens), lambda i, c: (0, i // chunks, 0, 0)),
            ],
            out_specs=[per_head, pl.BlockSpec((heads, 1, tokens), lambda i, c: (i, 0, 0))],
        ),
        compiler_params=pltpu.CompilerParams(vmem_limit_bytes=VMEM_LIMIT),
        cost_estimate=pl.CostEstimate(
            flops=16 * work * HD, bytes_accessed=8 * queries.size, transcendentals=work
        ),
        name="attend",
    )(index, queries, keys, values_t)


def attend_back(index, queries, d_out, out, lse, keys, values, keys_t):
    blocks, kv, tokens, _ = keys.shape
    q_rows = queries.shape[0]
    group = q_rows // HD // kv
    heads = heads_at_once(group)
    chunks = group // heads
    per_head = pl.BlockSpec((heads * HD, tokens), lambda i, c: (i, 0))
    natural = pl.BlockSpec((blocks, 1, tokens, HD), lambda i, c: (0, i // chunks, 0, 0))
    work = blocks * tokens * tokens * (q_rows // HD)
    return pl.pallas_call(
        functools.partial(attend_back_kernel, LOG2E / math.sqrt(HD), heads, chunks),
        out_shape=(
            jax.ShapeDtypeStruct(queries.shape, F32),
            jax.ShapeDtypeStruct(keys.shape, F32),
            jax.ShapeDtypeStruct(keys.shape, F32),
        ),
        grid_spec=pltpu.PrefetchScalarGridSpec(
            num_scalar_prefetch=1,
            grid=(kv * chunks,),
            in_specs=[
                per_head,
                per_head,
                per_head,
                pl.BlockSpec((heads, 1, tokens), lambda i, c: (i, 0, 0)),
                natural,
                natural,
                pl.BlockSpec((blocks, 1, HD, tokens), lambda i, c: (0, i // chunks, 0, 0)),
            ],
            out_specs=[per_head, natural, natural],
        ),
        compiler_params=pltpu.CompilerParams(vmem_limit_bytes=VMEM_LIMIT),
        cost_estimate=pl.CostEstimate(
            flops=40 * work * HD, bytes_accessed=16 * queries.size, transcendentals=work
        ),
        name="attend_back",
    )(index, queries, d_out, out, lse, keys, values, keys_t)


def norm_forward(hidden, gain):
    inverse = lax.rsqrt(jnp.mean(hidden * hidden, -1, keepdims=True) + EPS)
    normal = hidden * inverse
    return (normal, inverse, (normal * gain).astype(BF16))


def norm_backward(grad_normed, normal, inverse, gain):
    scaled = grad_normed * gain
    grad_in = inverse * (scaled - normal * jnp.mean(scaled * normal, -1, keepdims=True))
    return (grad_in, jnp.sum(grad_normed * normal, 0))


def after(value, *others):
    return lax.optimization_barrier((value, *others))[0]


def swap(value, axis, bit, size):
    return lax.ppermute(value, axis, [(i, i ^ bit) for i in range(size)])


def take(value, index, rows, dim):
    return lax.dynamic_slice_in_dim(value, index * rows, rows, dim)


def halves(value, dim):
    middle = value.shape[dim] // 2
    return [lax.slice_in_dim(value, 0, middle, axis=dim), lax.slice_in_dim(value, middle, None, axis=dim)]


class Plane:
    def __init__(self, size):
        self.size = size
        bits = [1 << i for i in range(size.bit_length() - 1)]
        assert 1 << len(bits) == size
        self.me = lax.axis_index("fsdp")
        self.bits = [bits, bits[::-1]]
        self.orders = []
        for part in self.bits:
            order = [0]
            for bit in part:
                order = order + [d ^ bit for d in order]
            self.orders.append(order)

    def gather(self, parts):
        found = list(parts)
        self.first_hop = None
        for bits in zip(*self.bits):
            found = [
                jnp.concatenate([have, swap(have, "fsdp", bit, self.size)], 0) for have, bit in zip(found, bits)
            ]
            found = list(lax.optimization_barrier(tuple(found)))
            if self.first_hop is None:
                self.first_hop = tuple(found)
        return found

    def scatter(self, parts):
        sums = list(parts)
        for bits in zip(*(bits[::-1] for bits in self.bits)):
            for part, bit in enumerate(bits):
                mine, away = halves(sums[part], 0)
                sums[part] = mine.astype(F32) + swap(away.astype(BF16), "fsdp", bit, self.size).astype(F32)
            sums = list(lax.optimization_barrier(tuple(sums)))
        return sums

    def exchange(self, blocks):
        return [swap(b, "fsdp", d, self.size) if d else b for d, b in enumerate(blocks)]

    def place(self, blocks, dim):
        rows = blocks[0].shape[dim]
        shape = list(blocks[0].shape)
        shape[dim] = rows * self.size
        whole = jnp.zeros(shape, blocks[0].dtype)
        for d, b in enumerate(blocks):
            whole = lax.dynamic_update_slice_in_dim(whole, b, (self.me ^ d) * rows, dim)
        return whole


def add_rounded(a, b):
    return lax.optimization_barrier((a.astype(F32) + b.astype(F32)).astype(a.dtype))


def line_side(axis):
    me = lax.axis_index(axis)
    return (me ^ (me >> 1)) & 1


def in_pairs(size):
    return size >= 4 and size & (size - 1) == 0


def line_start(values, axis, size):
    if not in_pairs(size):
        return [None] * len(values)
    side = line_side(axis)
    return [swap(take(v, 1 - side, v.shape[0] // 2, 0), axis, 1, size) for v in values]


def line_finish(values, first, axis, size):
    if size == 1:
        return values
    if not in_pairs(size):
        return [lax.psum(v, axis) for v in values]
    side = line_side(axis)
    sums = []
    for v, came in zip(values, first):
        total = add_rounded(take(v, side, v.shape[0] // 2, 0), came)
        reach = 3
        while reach < size:
            total = add_rounded(total, swap(total, axis, reach, size))
            reach = 2 * reach + 1
        other = swap(total, axis, 1, size)
        sums.append(
            jnp.concatenate([jnp.where(side == 0, total, other), jnp.where(side == 0, other, total)], 0)
        )
    return sums


def per_device(sizes, layer_input, cot, wq, wk, wv, wo, w_gate, w_up, w_down, gain_attn, gain_mlp):
    fsdp, ctx, tp = sizes
    assert tp == 2
    plane = Plane(fsdp)
    me_f, me_c, me_t = plane.me, lax.axis_index("ctx"), lax.axis_index("tp")
    partner = functools.partial(swap, axis="tp", bit=1, size=tp)
    begin = functools.partial(line_start, axis="ctx", size=ctx)
    finish = functools.partial(line_finish, axis="ctx", size=ctx)

    def line_sum(value):
        return finish([value], begin([value]))[0]

    block, width = layer_input.shape[1:]
    own_width = width // fsdp
    rows = block // tp
    units = w_gate.shape[1] // fsdp
    hidden_in = layer_input.reshape(block, width)
    upstream = cot.reshape(block, width)
    q_cols, kv_cols = wq.shape[1], wk.shape[1]
    kv_local = kv_cols // HD

    head_units = units // 128 * 128
    tail_units = units - head_units

    def units_of(weight, owner, dim):
        tails = lax.slice_in_dim(weight, fsdp * head_units, None, axis=dim)
        return jnp.concatenate(
            [take(weight, owner, head_units, dim), take(tails, owner, tail_units, dim)], dim
        )

    def place_units(blocks, dim):
        cut = lambda b, i, j: lax.slice_in_dim(b, i, j, axis=dim)
        heads = [cut(b, 0, head_units) for b in blocks]
        tails = [cut(b, head_units, units) for b in blocks]
        shape = list(blocks[0].shape)
        shape[dim] = units * fsdp
        whole = jnp.zeros(shape, blocks[0].dtype)
        for d, b in enumerate(heads):
            whole = lax.dynamic_update_slice_in_dim(whole, b, (me_f ^ d) * head_units, dim)
        return lax.dynamic_update_slice_in_dim(whole, plane.place(tails, dim), fsdp * head_units, dim)

    def both_rows(mine):
        other = partner(mine)
        first = me_t == 0
        return jnp.concatenate([jnp.where(first, mine, other), jnp.where(first, other, mine)], 0)

    def gather_tokens(mine):
        return jnp.concatenate(plane.gather(halves(mine, 0)), 0)

    def scatter_tokens(mine, away):
        total = mine + partner(away.astype(BF16)).astype(F32)
        return jnp.concatenate(plane.scatter(halves(total, 0)), 0)

    qkv_cols = q_cols + 2 * kv_cols
    gain_rows = 32 * -(-2 * own_width // (32 * qkv_cols))
    gains = jnp.concatenate([gain_attn, gain_mlp])
    gains = jnp.pad(gains, (0, gain_rows * qkv_cols - gains.size)).reshape(gain_rows, qkv_cols)
    w_own = jnp.concatenate([wq, wk, wv], 1)
    top = own_width // 2
    found = plane.gather([w_own[:top], jnp.concatenate([w_own[top:], gains], 0)])
    w_qkv = jnp.zeros((width, qkv_cols), BF16)
    gains_all = jnp.zeros((fsdp, gain_rows * qkv_cols), BF16)
    for have, order, tall, first in zip(found, plane.orders, (top, own_width - top + gain_rows), (0, top)):
        for i, d in enumerate(order):
            blk = have[i * tall : (i + 1) * tall]
            owner = me_f ^ d
            if first:
                gains_all = lax.dynamic_update_slice_in_dim(
                    gains_all, blk[own_width - top :].reshape(1, -1), owner, 0
                )
                blk = blk[: own_width - top]
            w_qkv = lax.dynamic_update_slice_in_dim(w_qkv, blk, owner * own_width + first, 0)
    gain_first = gains_all[:, :own_width].reshape(width).astype(F32)
    gain_second = gains_all[:, own_width : 2 * own_width].reshape(width).astype(F32)

    positions = me_c * block + jnp.arange(block, dtype=jnp.int32)
    cosine, sine = rope_tables(positions, HD)
    normal_one, inv_one, normed_one = norm_forward(hidden_in, gain_first)
    qkv = dot(w_qkv, normed_one, (0, 1))
    turned = rope(qkv[: q_cols + kv_cols], cosine, sine).astype(BF16)
    queries = turned[:q_cols]
    kv_own = jnp.concatenate([turned[q_cols:], qkv[q_cols + kv_cols :].astype(BF16)], 0)
    kv_seq = jnp.stack(
        [kv_own]
        + [lax.ppermute(kv_own, "ctx", [(i, i + d) for i in range(ctx - d)]) for d in range(1, ctx)]
    ).reshape(ctx, 2, kv_local, HD, block)
    keys_t, values_t = kv_seq[:, 0], kv_seq[:, 1]
    keys, values = jnp.swapaxes(keys_t, 2, 3), jnp.swapaxes(values_t, 2, 3)

    ready = lax.optimization_barrier((found[0], found[1]))[0]
    w_out_blocks = plane.exchange([after(wo, ready)] * fsdp)
    w_out = plane.place(w_out_blocks, 1)
    w_gate, w_up = after(w_gate, *plane.first_hop), after(w_up, *plane.first_hop)
    gate_up = plane.exchange(
        [
            after(jnp.concatenate([units_of(w_gate, me_f ^ d, 1), units_of(w_up, me_f ^ d, 1)], 0), ready)
            for d in range(fsdp)
        ]
    )
    index = me_c.astype(jnp.int32).reshape(1)
    context, lse = attend(index, queries, keys, values_t)
    attn_part = dot(context, w_out, (0, 0))
    attn_part, *gate_up = lax.optimization_barrier((attn_part, *gate_up))
    gate_mine = plane.place([b[:own_width] for b in gate_up], 0)
    up_mine = plane.place([b[own_width:] for b in gate_up], 0)
    mid = (
        take(hidden_in, me_t, rows, 0)
        + take(attn_part, me_t, rows, 0)
        + partner(take(attn_part, 1 - me_t, rows, 0))
    )

    normal_two, inv_two, normed_two = norm_forward(mid, gain_second)
    two_mine = gather_tokens(normed_two)
    first_hop = plane.first_hop or ()
    two_all = jnp.concatenate([two_mine, partner(two_mine)], 0)
    cot_own = after(take(upstream, me_t, rows, 0).astype(BF16), *first_hop)
    cot_mine = gather_tokens(cot_own)
    cot_all = jnp.concatenate([cot_mine, partner(cot_mine)], 0)
    down_mine = plane.place(
        plane.exchange([after(units_of(w_down, me_f ^ d, 0), *first_hop) for d in range(fsdp)]), 1
    )
    gate = dot(two_all, gate_mine, (1, 0))
    up = dot(two_all, up_mine, (1, 0))
    sig = jax.nn.sigmoid(gate)
    silu = gate * sig
    act = (silu * up).astype(BF16)
    d_act = dot(cot_all, down_mine, (1, 1))
    d_gate = (d_act * up * sig * (1.0 + gate * (1.0 - sig))).astype(BF16)
    d_up = (d_act * silu).astype(BF16)

    def grads_of(owner):
        columns = take(two_all, owner, own_width, 1)
        both = [dot(columns, right, (0, 0)).astype(BF16) for right in (d_gate, d_up)]
        return jnp.concatenate(both, 0)

    gu_local = [grads_of(me_f ^ d) for d in range(fsdp)]
    d_gate, d_up, *gu_local = lax.optimization_barrier((d_gate, d_up, *gu_local))
    gu_grads = plane.exchange(gu_local)
    dn_away, dn_mine = [
        dot(g, gate_mine, (1, 1)) + dot(u, up_mine, (1, 1))
        for g, u in zip(halves(d_gate, 0)[::-1], halves(d_up, 0)[::-1])
    ]
    dn_total = dn_mine + partner(dn_away.astype(BF16)).astype(F32)
    dn_total, *gu_grads = lax.optimization_barrier((dn_total, *gu_grads))
    dn_two = jnp.concatenate(plane.scatter(halves(dn_total, 0)), 0)
    gu_whole = [
        place_units([b[i:j] for b in gu_grads], 1) for i, j in ((0, own_width), (own_width, 2 * own_width))
    ]
    gu_first = begin(gu_whole)

    back_two, gain_two_grad = norm_backward(dn_two, normal_two, inv_two, gain_second)
    dmid = take(upstream, me_t, rows, 0) + back_two
    dmid_b = both_rows(dmid.astype(BF16))
    d_context = dot(w_out, dmid_b, (1, 1)).astype(BF16)

    act, cot_all, d_context = lax.optimization_barrier((act, cot_all, d_context))
    down_local = [dot(act, take(cot_all, me_f ^ d, own_width, 1), (0, 0)).astype(BF16) for d in range(fsdp)]
    out_grads = [
        [dot(context[i:j], take(dmid_b, me_f ^ d, own_width, 1), (1, 0)) for d in order]
        for (i, j), order in zip(((0, q_cols // 2), (q_cols // 2, q_cols)), plane.orders)
    ]
    d_context, *down_local = lax.optimization_barrier((d_context, *down_local))
    d_context, gu_first[0], *gu_whole = lax.optimization_barrier((d_context, gu_first[0], *gu_whole))
    down_grads = plane.exchange(down_local)
    dwo_parts = plane.scatter([jnp.concatenate(g, 0) for g in out_grads])

    dq_rot, dk_seq, dv_seq = attend_back(index, queries, d_context, context, lse, keys, values, keys_t)
    dq_rot, gu_first[1] = lax.optimization_barrier((dq_rot, gu_first[1]))
    dw_gate, dw_up = [v.astype(F32) for v in finish(gu_whole, gu_first)]
    dw_down = line_sum(place_units(down_grads, 0)).astype(F32)
    scale = 1.0 / math.sqrt(HD)
    dkv_seq = jnp.swapaxes(jnp.concatenate([dk_seq * scale, dv_seq], 1), 2, 3)
    dkv_seq = dkv_seq.reshape(ctx, 2 * kv_cols, block)
    dkv_sent = dkv_seq.astype(BF16)
    dkv = dkv_seq[0]
    for d in range(1, ctx):
        came = lax.ppermute(dkv_sent[d], "ctx", [(i + d, i) for i in range(ctx - d)])
        dkv = dkv + came.astype(F32)
    d_turned = rope(jnp.concatenate([dq_rot * scale, dkv[:kv_cols]], 0), cosine, -sine)
    d_qkv = jnp.concatenate([d_turned, dkv[kv_cols:]], 0).astype(BF16)

    qkv_grads = plane.scatter(
        [
            jnp.concatenate(
                [
                    dot(lax.dynamic_slice_in_dim(normed_one, (me_f ^ d) * own_width + first, tall, 1), d_qkv, (0, 1))
                    for d in order
                ],
                0,
            )
            for first, tall, order in zip((0, top), (top, own_width - top), plane.orders)
        ]
    )
    dwo = line_sum(jnp.concatenate(dwo_parts, 0).astype(BF16)).astype(F32)
    dn_part_one = dot(d_qkv, w_qkv, (0, 1))
    dn_one = take(dn_part_one, me_t, rows, 0) + partner(
        take(dn_part_one, 1 - me_t, rows, 0).astype(BF16)
    ).astype(F32)
    back_one, gain_one_grad = norm_backward(
        dn_one, take(normal_one, me_t, rows, 0), take(inv_one, me_t, rows, 0), gain_first
    )
    dx_local = both_rows(dmid + back_one)

    act_late = after(act, dq_rot)
    mlp_mine, mlp_away = [dot(a, down_mine, (1, 0)) for a in halves(act_late, 0)]
    out_local = both_rows(mid + scatter_tokens(mlp_mine, mlp_away))

    gain_grads = jnp.stack([gain_one_grad, gain_two_grad])
    gain_grads = gain_grads + partner(gain_grads)
    gain_blocks = [take(gain_grads, me_f ^ d, own_width, 1) for d in range(fsdp)]
    gain_own = functools.reduce(jnp.add, plane.exchange(gain_blocks)).reshape(-1)
    gain_own = jnp.pad(gain_own, (0, gain_rows * qkv_cols - gain_own.size)).reshape(gain_rows, qkv_cols)
    qkv_sum = line_sum(jnp.concatenate([*qkv_grads, gain_own], 0).astype(BF16)).astype(F32)
    dw_qkv = qkv_sum[:own_width]
    gain_sum = qkv_sum[own_width:].reshape(-1)[: 2 * own_width].reshape(2, own_width)
    return (
        out_local.reshape(1, block, width),
        dx_local.reshape(1, block, width),
        dw_qkv[:, :q_cols],
        dw_qkv[:, q_cols : q_cols + kv_cols],
        dw_qkv[:, q_cols + kv_cols :],
        dwo,
        dw_gate,
        dw_up,
        dw_down,
        gain_sum[0],
        gain_sum[1],
    )


def solution(mesh):
    tokens = P("fsdp", "ctx", None)
    rows, columns = P("fsdp", "tp"), P("tp", "fsdp")
    weights = (rows, rows, rows, columns, rows, rows, columns, P("fsdp"), P("fsdp"))
    sizes = tuple(mesh.shape[name] for name in ("fsdp", "ctx", "tp"))
    return jax.shard_map(
        functools.partial(per_device, sizes),
        mesh=mesh,
        in_specs=(tokens, tokens, *weights),
        out_specs=(tokens, tokens, *weights),
        check_vma=False,
    )
```

```python
import functools
import math

import jax
import jax.numpy as jnp
from jax import lax
from jax.experimental import pallas as pl
from jax.experimental.pallas import tpu as pltpu
from jax.sharding import PartitionSpec as P

HD = 64
EPS = 1e-05
ROPE_BASE = 10000.0
NEG_BIG = -1e30
F32 = jnp.float32
BF16 = jnp.bfloat16


LOG2E = 1.4426950408889634
VMEM_LIMIT = 56 * 1024 * 1024


def rope_tables(positions, head_dim):
    half = head_dim // 2
    freq = ROPE_BASE ** (-(jnp.arange(half, dtype=F32) * 2.0 / head_dim))
    angles = positions.astype(F32)[None, :] * freq[:, None]
    return (jnp.cos(angles), jnp.sin(angles))


def rope(values, cosine, sine):
    rows, tokens = values.shape
    first, second = jnp.moveaxis(values.reshape(rows // HD, 2, HD // 2, tokens), 1, 0)
    turned = [first * cosine - second * sine, second * cosine + first * sine]
    return jnp.stack(turned, 1).reshape(rows, tokens)


def dot(left, right, dims):
    return lax.dot_general(left, right, ((dims[:1], dims[1:]), ((), ())), preferred_element_type=F32)


def causal(shape):
    keys = lax.broadcasted_iota(jnp.int32, shape, 0)
    return keys <= lax.broadcasted_iota(jnp.int32, shape, 1)


def attend_kernel(factor, heads, index, q_ref, k_ref, vt_ref, out_ref, lse_ref):
    last = index[0]

    def step(back, carry, masked):
        after_step = []
        for h, (top, total, accum) in enumerate(carry):
            scores = dot(k_ref[back, 0], q_ref[pl.ds(h * HD, HD), :], (1, 0))
            if masked:
                scores = jnp.where(causal(scores.shape), scores, NEG_BIG)
            newest = jnp.maximum(top, jnp.max(scores, 0, keepdims=True))
            probs = jnp.exp2((scores - newest) * factor)
            fade = jnp.exp2((top - newest) * factor)
            total = total * fade + jnp.sum(probs, 0, keepdims=True)
            accum = accum * fade + dot(vt_ref[back, 0], probs.astype(BF16), (1, 0))
            after_step.append((newest, total, accum))
        return tuple(after_step)

    tokens = q_ref.shape[1]
    row = jnp.zeros((1, tokens), F32)
    carry = tuple((row + NEG_BIG, row, jnp.zeros((HD, tokens), F32)) for _ in range(heads))
    carry = step(0, carry, True)
    carry = lax.fori_loop(1, last + 1, functools.partial(step, masked=False), carry)
    for h, (top, total, accum) in enumerate(carry):
        out_ref[pl.ds(h * HD, HD), :] = (accum / total).astype(BF16)
        lse_ref[h] = top * factor + jnp.log(total) * LOG2E


def attend_back_kernel(
    factor, heads, chunks, index, q_ref, do_ref, o_ref, lse_ref, k_ref, v_ref, kt_ref, dq_ref, dk_ref, dv_ref
):
    last = index[0]
    rows = [pl.ds(h * HD, HD) for h in range(heads)]
    deltas = [
        jnp.sum(do_ref[r, :].astype(F32) * o_ref[r, :].astype(F32), 0, keepdims=True) for r in rows
    ]

    @pl.when(pl.program_id(0) % chunks == 0)
    def _():
        dk_ref[...] = jnp.zeros_like(dk_ref)
        dv_ref[...] = jnp.zeros_like(dv_ref)

    def step(back, masked):
        dk, dv = dk_ref[back, 0], dv_ref[back, 0]
        for h, r in enumerate(rows):
            q, do = q_ref[r, :], do_ref[r, :]
            scores = dot(k_ref[back, 0], q, (1, 0))
            probs = jnp.exp2(scores * factor - lse_ref[h])
            if masked:
                probs = jnp.where(causal(scores.shape), probs, 0.0)
            dv = dv + dot(probs.astype(BF16), do, (1, 1))
            dprobs = dot(v_ref[back, 0], do, (1, 0))
            dscores = (probs * (dprobs - deltas[h])).astype(BF16)
            dk = dk + dot(dscores, q, (1, 1))
            dq = dot(kt_ref[back, 0], dscores, (1, 0))
            if masked:
                dq_ref[r, :] = dq
            else:
                dq_ref[r, :] += dq
        dk_ref[back, 0] = dk
        dv_ref[back, 0] = dv

    step(0, True)

    def body(back, carry):
        step(back, False)
        return carry

    lax.fori_loop(1, last + 1, body, 0)


def heads_at_once(group):
    return max(n for n in (4, 2, 1) if group % n == 0)


def attend(index, queries, keys, values_t):
    blocks, kv, tokens, _ = keys.shape
    q_rows = queries.shape[0]
    group = q_rows // HD // kv
    heads = heads_at_once(group)
    chunks = group // heads
    per_head = pl.BlockSpec((heads * HD, tokens), lambda i, c: (i, 0))
    work = blocks * tokens * tokens * (q_rows // HD)
    return pl.pallas_call(
        functools.partial(attend_kernel, LOG2E / math.sqrt(HD), heads),
        out_shape=(
            jax.ShapeDtypeStruct(queries.shape, BF16),
            jax.ShapeDtypeStruct((q_rows // HD, 1, tokens), F32),
        ),
        grid_spec=pltpu.PrefetchScalarGridSpec(
            num_scalar_prefetch=1,
            grid=(kv * chunks,),
            in_specs=[
                per_head,
                pl.BlockSpec((blocks, 1, tokens, HD), lambda i, c: (0, i // chunks, 0, 0)),
                pl.BlockSpec((blocks, 1, HD, tokens), lambda i, c: (0, i // chunks, 0, 0)),
            ],
            out_specs=[per_head, pl.BlockSpec((heads, 1, tokens), lambda i, c: (i, 0, 0))],
        ),
        compiler_params=pltpu.CompilerParams(vmem_limit_bytes=VMEM_LIMIT),
        cost_estimate=pl.CostEstimate(
            flops=16 * work * HD, bytes_accessed=8 * queries.size, transcendentals=work
        ),
        name="attend",
    )(index, queries, keys, values_t)


def attend_back(index, queries, d_out, out, lse, keys, values, keys_t):
    blocks, kv, tokens, _ = keys.shape
    q_rows = queries.shape[0]
    group = q_rows // HD // kv
    heads = heads_at_once(group)
    chunks = group // heads
    per_head = pl.BlockSpec((heads * HD, tokens), lambda i, c: (i, 0))
    natural = pl.BlockSpec((blocks, 1, tokens, HD), lambda i, c: (0, i // chunks, 0, 0))
    work = blocks * tokens * tokens * (q_rows // HD)
    return pl.pallas_call(
        functools.partial(attend_back_kernel, LOG2E / math.sqrt(HD), heads, chunks),
        out_shape=(
            jax.ShapeDtypeStruct(queries.shape, F32),
            jax.ShapeDtypeStruct(keys.shape, F32),
            jax.ShapeDtypeStruct(keys.shape, F32),
        ),
        grid_spec=pltpu.PrefetchScalarGridSpec(
            num_scalar_prefetch=1,
            grid=(kv * chunks,),
            in_specs=[
                per_head,
                per_head,
                per_head,
                pl.BlockSpec((heads, 1, tokens), lambda i, c: (i, 0, 0)),
                natural,
                natural,
                pl.BlockSpec((blocks, 1, HD, tokens), lambda i, c: (0, i // chunks, 0, 0)),
            ],
            out_specs=[per_head, natural, natural],
        ),
        compiler_params=pltpu.CompilerParams(vmem_limit_bytes=VMEM_LIMIT),
        cost_estimate=pl.CostEstimate(
            flops=40 * work * HD, bytes_accessed=16 * queries.size, transcendentals=work
        ),
        name="attend_back",
    )(index, queries, d_out, out, lse, keys, values, keys_t)


def norm_forward(hidden, gain):
    inverse = lax.rsqrt(jnp.mean(hidden * hidden, -1, keepdims=True) + EPS)
    normal = hidden * inverse
    return (normal, inverse, (normal * gain).astype(BF16))


def norm_backward(grad_normed, normal, inverse, gain):
    scaled = grad_normed * gain
    grad_in = inverse * (scaled - normal * jnp.mean(scaled * normal, -1, keepdims=True))
    return (grad_in, jnp.sum(grad_normed * normal, 0))


def after(value, *others):
    return lax.optimization_barrier((value, *others))[0]


def swap(value, axis, bit, size):
    return lax.ppermute(value, axis, [(i, i ^ bit) for i in range(size)])


def take(value, index, rows, dim):
    return lax.dynamic_slice_in_dim(value, index * rows, rows, dim)


def halves(value, dim):
    middle = value.shape[dim] // 2
    return [lax.slice_in_dim(value, 0, middle, axis=dim), lax.slice_in_dim(value, middle, None, axis=dim)]


class Plane:
    def __init__(self, size):
        self.size = size
        bits = [1 << i for i in range(size.bit_length() - 1)]
        assert 1 << len(bits) == size
        self.me = lax.axis_index("fsdp")
        self.bits = [bits, bits[::-1]]
        self.orders = []
        for part in self.bits:
            order = [0]
            for bit in part:
                order = order + [d ^ bit for d in order]
            self.orders.append(order)

    def gather(self, parts):
        found = list(parts)
        self.first_hop = None
        for bits in zip(*self.bits):
            found = [
                jnp.concatenate([have, swap(have, "fsdp", bit, self.size)], 0) for have, bit in zip(found, bits)
            ]
            found = list(lax.optimization_barrier(tuple(found)))
            if self.first_hop is None:
                self.first_hop = tuple(found)
        return found

    def scatter(self, parts):
        sums = list(parts)
        self.first_sums = None
        for bits in zip(*(bits[::-1] for bits in self.bits)):
            for part, bit in enumerate(bits):
                mine, away = halves(sums[part], 0)
                sums[part] = mine.astype(F32) + swap(away.astype(BF16), "fsdp", bit, self.size).astype(F32)
            sums = list(lax.optimization_barrier(tuple(sums)))
            if self.first_sums is None:
                self.first_sums = tuple(sums)
        return sums

    def exchange(self, blocks):
        return [swap(b, "fsdp", d, self.size) if d else b for d, b in enumerate(blocks)]

    def place(self, blocks, dim):
        rows = blocks[0].shape[dim]
        shape = list(blocks[0].shape)
        shape[dim] = rows * self.size
        whole = jnp.zeros(shape, blocks[0].dtype)
        for d, b in enumerate(blocks):
            whole = lax.dynamic_update_slice_in_dim(whole, b, (self.me ^ d) * rows, dim)
        return whole


def add_rounded(a, b):
    return lax.optimization_barrier((a.astype(F32) + b.astype(F32)).astype(a.dtype))


def line_side(axis):
    me = lax.axis_index(axis)
    return (me ^ (me >> 1)) & 1


def in_pairs(size):
    return size >= 4 and size & (size - 1) == 0


def line_start(values, axis, size):
    if not in_pairs(size):
        return [None] * len(values)
    side = line_side(axis)
    return [swap(take(v, 1 - side, v.shape[0] // 2, 0), axis, 1, size) for v in values]


def line_finish(values, first, axis, size):
    if size == 1:
        return values
    if not in_pairs(size):
        return [lax.psum(v, axis) for v in values]
    side = line_side(axis)
    sums = []
    for v, came in zip(values, first):
        total = add_rounded(take(v, side, v.shape[0] // 2, 0), came)
        reach = 3
        while reach < size:
            total = add_rounded(total, swap(total, axis, reach, size))
            reach = 2 * reach + 1
        other = swap(total, axis, 1, size)
        sums.append(
            jnp.concatenate([jnp.where(side == 0, total, other), jnp.where(side == 0, other, total)], 0)
        )
    return sums


def per_device(sizes, layer_input, cot, wq, wk, wv, wo, w_gate, w_up, w_down, gain_attn, gain_mlp):
    fsdp, ctx, tp = sizes
    assert tp == 2
    plane = Plane(fsdp)
    me_f, me_c, me_t = plane.me, lax.axis_index("ctx"), lax.axis_index("tp")
    partner = functools.partial(swap, axis="tp", bit=1, size=tp)
    begin = functools.partial(line_start, axis="ctx", size=ctx)
    finish = functools.partial(line_finish, axis="ctx", size=ctx)

    def line_sum(value):
        return finish([value], begin([value]))[0]

    block, width = layer_input.shape[1:]
    own_width = width // fsdp
    rows = block // tp
    units = w_gate.shape[1] // fsdp
    hidden_in = layer_input.reshape(block, width)
    upstream = cot.reshape(block, width)
    q_cols, kv_cols = wq.shape[1], wk.shape[1]
    kv_local = kv_cols // HD

    head_units = units // 128 * 128
    tail_units = units - head_units

    def units_of(weight, owner, dim):
        tails = lax.slice_in_dim(weight, fsdp * head_units, None, axis=dim)
        return jnp.concatenate(
            [take(weight, owner, head_units, dim), take(tails, owner, tail_units, dim)], dim
        )

    def place_units(blocks, dim):
        cut = lambda b, i, j: lax.slice_in_dim(b, i, j, axis=dim)
        heads = [cut(b, 0, head_units) for b in blocks]
        tails = [cut(b, head_units, units) for b in blocks]
        shape = list(blocks[0].shape)
        shape[dim] = units * fsdp
        whole = jnp.zeros(shape, blocks[0].dtype)
        for d, b in enumerate(heads):
            whole = lax.dynamic_update_slice_in_dim(whole, b, (me_f ^ d) * head_units, dim)
        return lax.dynamic_update_slice_in_dim(whole, plane.place(tails, dim), fsdp * head_units, dim)

    def both_rows(mine):
        other = partner(mine)
        first = me_t == 0
        return jnp.concatenate([jnp.where(first, mine, other), jnp.where(first, other, mine)], 0)

    def gather_tokens(mine):
        return jnp.concatenate(plane.gather(halves(mine, 0)), 0)

    def scatter_tokens(mine, away):
        total = mine + partner(away.astype(BF16)).astype(F32)
        return jnp.concatenate(plane.scatter(halves(total, 0)), 0)

    qkv_cols = q_cols + 2 * kv_cols
    gain_rows = 32 * -(-2 * own_width // (32 * qkv_cols))
    gains = jnp.concatenate([gain_attn, gain_mlp])
    gains = jnp.pad(gains, (0, gain_rows * qkv_cols - gains.size)).reshape(gain_rows, qkv_cols)
    w_own = jnp.concatenate([wq, wk, wv], 1)
    top = own_width // 2
    found = plane.gather([w_own[:top], jnp.concatenate([w_own[top:], gains], 0)])
    w_qkv = jnp.zeros((width, qkv_cols), BF16)
    assert 2 * own_width <= qkv_cols
    gains_all = jnp.zeros((fsdp, 2 * own_width), BF16)
    for have, order, tall, first in zip(found, plane.orders, (top, own_width - top + gain_rows), (0, top)):
        for i, d in enumerate(order):
            blk = have[i * tall : (i + 1) * tall]
            owner = me_f ^ d
            if first:
                line = blk[own_width - top : own_width - top + 1, : 2 * own_width]
                gains_all = lax.dynamic_update_slice_in_dim(gains_all, line, owner, 0)
                blk = blk[: own_width - top]
            w_qkv = lax.dynamic_update_slice_in_dim(w_qkv, blk, owner * own_width + first, 0)
    gain_first = gains_all[:, :own_width].reshape(width).astype(F32)
    gain_second = gains_all[:, own_width : 2 * own_width].reshape(width).astype(F32)

    positions = me_c * block + jnp.arange(block, dtype=jnp.int32)
    cosine, sine = rope_tables(positions, HD)
    normal_one, inv_one, normed_one = norm_forward(hidden_in, gain_first)
    qkv = dot(w_qkv, normed_one, (0, 1))
    turned = rope(qkv[: q_cols + kv_cols], cosine, sine).astype(BF16)
    queries = turned[:q_cols]
    kv_own = jnp.concatenate([turned[q_cols:], qkv[q_cols + kv_cols :].astype(BF16)], 0)
    kv_seq = jnp.stack(
        [kv_own]
        + [lax.ppermute(kv_own, "ctx", [(i, i + d) for i in range(ctx - d)]) for d in range(1, ctx)]
    ).reshape(ctx, 2, kv_local, HD, block)
    keys_t, values_t = kv_seq[:, 0], kv_seq[:, 1]
    keys, values = jnp.swapaxes(keys_t, 2, 3), jnp.swapaxes(values_t, 2, 3)

    ready = lax.optimization_barrier((found[0], found[1]))[0]
    w_out_blocks = plane.exchange([after(wo, ready)] * fsdp)
    w_out = plane.place(w_out_blocks, 1)
    w_gate, w_up = after(w_gate, *plane.first_hop), after(w_up, *plane.first_hop)
    gate_up = plane.exchange(
        [
            after(jnp.concatenate([units_of(w_gate, me_f ^ d, 1), units_of(w_up, me_f ^ d, 1)], 0), ready)
            for d in range(fsdp)
        ]
    )
    index = me_c.astype(jnp.int32).reshape(1)
    context, lse = attend(index, queries, keys, values_t)
    attn_part = dot(context, w_out, (0, 0))
    attn_part, *gate_up = lax.optimization_barrier((attn_part, *gate_up))
    gate_mine = plane.place([b[:own_width] for b in gate_up], 0)
    up_mine = plane.place([b[own_width:] for b in gate_up], 0)
    mid = (
        take(hidden_in, me_t, rows, 0)
        + take(attn_part, me_t, rows, 0)
        + partner(take(attn_part, 1 - me_t, rows, 0))
    )

    normal_two, inv_two, normed_two = norm_forward(mid, gain_second)
    two_mine = gather_tokens(normed_two)
    first_hop = plane.first_hop or ()
    two_all = jnp.concatenate([two_mine, partner(two_mine)], 0)
    cot_own = after(take(upstream, me_t, rows, 0).astype(BF16), *first_hop)
    cot_mine = gather_tokens(cot_own)
    gate = dot(two_all, gate_mine, (1, 0))
    up = dot(two_all, up_mine, (1, 0))
    down_blocks = plane.exchange([after(units_of(w_down, me_f ^ d, 0), *first_hop) for d in range(fsdp)])
    gate, up, cot_mine, *down_blocks = lax.optimization_barrier((gate, up, cot_mine, *down_blocks))
    cot_all = jnp.concatenate([cot_mine, partner(cot_mine)], 0)
    down_mine = plane.place(down_blocks, 1)
    sig = jax.nn.sigmoid(gate)
    silu = gate * sig
    act = (silu * up).astype(BF16)
    d_act = dot(cot_all, down_mine, (1, 1))
    d_gate = (d_act * up * sig * (1.0 + gate * (1.0 - sig))).astype(BF16)
    d_up = (d_act * silu).astype(BF16)

    def grads_of(owner):
        columns = take(two_all, owner, own_width, 1)
        both = [dot(columns, right, (0, 0)).astype(BF16) for right in (d_gate, d_up)]
        return jnp.concatenate(both, 0)

    gu_local = [grads_of(me_f ^ d) for d in range(fsdp)]
    d_gate, d_up, *gu_local = lax.optimization_barrier((d_gate, d_up, *gu_local))
    gu_grads = plane.exchange(gu_local)
    dn_away, dn_mine = [
        dot(g, gate_mine, (1, 1)) + dot(u, up_mine, (1, 1))
        for g, u in zip(halves(d_gate, 0)[::-1], halves(d_up, 0)[::-1])
    ]
    dn_total = dn_mine + partner(dn_away.astype(BF16)).astype(F32)
    dn_two = jnp.concatenate(plane.scatter(halves(dn_total, 0)), 0)
    gu_grads = [after(g, *(plane.first_sums or ())) for g in gu_grads]
    gu_whole = [
        place_units([b[i:j] for b in gu_grads], 1) for i, j in ((0, own_width), (own_width, 2 * own_width))
    ]
    gu_first = begin(gu_whole)

    back_two, gain_two_grad = norm_backward(dn_two, normal_two, inv_two, gain_second)
    dmid = take(upstream, me_t, rows, 0) + back_two
    dmid_b = both_rows(dmid.astype(BF16))
    d_context = dot(w_out, dmid_b, (1, 1)).astype(BF16)

    act, cot_all, d_context = lax.optimization_barrier((act, cot_all, d_context))
    down_local = [dot(act, take(cot_all, me_f ^ d, own_width, 1), (0, 0)).astype(BF16) for d in range(fsdp)]
    out_grads = [
        [dot(context[i:j], take(dmid_b, me_f ^ d, own_width, 1), (1, 0)) for d in order]
        for (i, j), order in zip(((0, q_cols // 2), (q_cols // 2, q_cols)), plane.orders)
    ]
    d_context, *down_local = lax.optimization_barrier((d_context, *down_local))
    d_context, gu_first[0], *gu_whole = lax.optimization_barrier((d_context, gu_first[0], *gu_whole))
    down_grads = plane.exchange(down_local)
    dwo_parts = plane.scatter([jnp.concatenate(g, 0) for g in out_grads])

    dq_rot, dk_seq, dv_seq = attend_back(index, queries, d_context, context, lse, keys, values, keys_t)
    dq_rot, gu_first[1] = lax.optimization_barrier((dq_rot, gu_first[1]))
    dw_gate, dw_up = [v.astype(F32) for v in finish(gu_whole, gu_first)]
    dw_down = line_sum(place_units(down_grads, 0)).astype(F32)
    scale = 1.0 / math.sqrt(HD)
    dkv_seq = jnp.swapaxes(jnp.concatenate([dk_seq * scale, dv_seq], 1), 2, 3)
    dkv_seq = dkv_seq.reshape(ctx, 2 * kv_cols, block)
    dkv_sent = dkv_seq.astype(BF16)
    dkv = dkv_seq[0]
    for d in range(1, ctx):
        came = lax.ppermute(dkv_sent[d], "ctx", [(i + d, i) for i in range(ctx - d)])
        dkv = dkv + came.astype(F32)
    d_turned = rope(jnp.concatenate([dq_rot * scale, dkv[:kv_cols]], 0), cosine, -sine)
    d_qkv = jnp.concatenate([d_turned, dkv[kv_cols:]], 0).astype(BF16)

    qkv_grads = plane.scatter(
        [
            jnp.concatenate(
                [
                    dot(lax.dynamic_slice_in_dim(normed_one, (me_f ^ d) * own_width + first, tall, 1), d_qkv, (0, 1))
                    for d in order
                ],
                0,
            )
            for first, tall, order in zip((0, top), (top, own_width - top), plane.orders)
        ]
    )
    dwo = line_sum(jnp.concatenate(dwo_parts, 0).astype(BF16)).astype(F32)
    dn_part_one = dot(d_qkv, w_qkv, (0, 1))
    dn_one = take(dn_part_one, me_t, rows, 0) + partner(
        take(dn_part_one, 1 - me_t, rows, 0).astype(BF16)
    ).astype(F32)
    back_one, gain_one_grad = norm_backward(
        dn_one, take(normal_one, me_t, rows, 0), take(inv_one, me_t, rows, 0), gain_first
    )
    dx_local = both_rows(dmid + back_one)

    act_late = after(act, dq_rot)
    mlp_mine, mlp_away = [dot(a, down_mine, (1, 0)) for a in halves(act_late, 0)]
    out_local = both_rows(mid + scatter_tokens(mlp_mine, mlp_away))

    gain_grads = jnp.stack([gain_one_grad, gain_two_grad])
    gain_grads = gain_grads + partner(gain_grads)
    gain_blocks = [take(gain_grads, me_f ^ d, own_width, 1) for d in range(fsdp)]
    gain_own = functools.reduce(jnp.add, plane.exchange(gain_blocks)).reshape(-1)
    gain_own = jnp.pad(gain_own, (0, gain_rows * qkv_cols - gain_own.size)).reshape(gain_rows, qkv_cols)
    qkv_sum = line_sum(jnp.concatenate([*qkv_grads, gain_own], 0).astype(BF16)).astype(F32)
    dw_qkv = qkv_sum[:own_width]
    gain_sum = qkv_sum[own_width:].reshape(-1)[: 2 * own_width].reshape(2, own_width)
    return (
        out_local.reshape(1, block, width),
        dx_local.reshape(1, block, width),
        dw_qkv[:, :q_cols],
        dw_qkv[:, q_cols : q_cols + kv_cols],
        dw_qkv[:, q_cols + kv_cols :],
        dwo,
        dw_gate,
        dw_up,
        dw_down,
        gain_sum[0],
        gain_sum[1],
    )


def solution(mesh):
    tokens = P("fsdp", "ctx", None)
    rows, columns = P("fsdp", "tp"), P("tp", "fsdp")
    weights = (rows, rows, rows, columns, rows, rows, columns, P("fsdp"), P("fsdp"))
    sizes = tuple(mesh.shape[name] for name in ("fsdp", "ctx", "tp"))
    return jax.shard_map(
        functools.partial(per_device, sizes),
        mesh=mesh,
        in_specs=(tokens, tokens, *weights),
        out_specs=(tokens, tokens, *weights),
        check_vma=False,
    )
```
